32 devices in a mesh: seq: 8 (over z, y), tp: 4 (over x, core).
Axes of the slice: x: 2, y: 2, z: 4, core: 2. Of those that a mesh axis runs over, the one named last changes fastest.
Arguments:
- queries: bfloat16 [768, 4096], P('seq', 'tp'), may hold values from -8 to 8
- keys: bfloat16 [768, 1024], P('seq', 'tp'), may hold values from -7 to 7
- values: bfloat16 [768, 1024], P('seq', 'tp'), may hold values from -24 to 24
- router_prob: float32 [768], P('seq'), may hold values from 0.2 to 1
- norm_gain: float32 [4096], P('tp'), may hold values from 0.25 to 1.75
- slot_pos: int32 [768], P('seq'), may hold values from 0 to 255, as said below
- live_count: int32 [8], P('seq'), may hold values from 1 to 96, 256 in all
Outputs:
- routed: bfloat16 [2048, 4096], P('seq', 'tp')
The draws below stay inside these ranges and needn't reach their ends.
Inputs may be any that keep to these rules, and one draw needn't show every extreme that they name: The slots of a shard that are live are its first live_count slots; the counts add up to 256 and the largest is 96. Within each shard's 96 slots the positions are distinct and ascending; slot a of shard s stands for the token s * 256 + slot_pos[a].
All inputs are finite; a program needn't handle non-finite values.
Results may differ from the reference program's by a relative error of at most 0.007.
Values may be sent and summed in bfloat16 or wider, within the bound.
A program may use at most 64 MiB of HBM per device.

```python
import math
import jax
import jax.numpy as jnp
import numpy as np
from jax import lax

H = 32
KVH = 8
HD = 128
TOK_DEV = 256
CAP = 96
SLOTS = 768
SELECTED = 256
TOKENS = 2048
N_SEQ = 8


def draw_queries(key, part):
    noise_key = jax.random.fold_in(key, 11)
    drawn = jnp.clip(jax.random.normal(noise_key, (SLOTS, H * HD), jnp.float32), -4.0, 4.0)
    return drawn.astype(jnp.bfloat16)


def draw_keys(key, part):
    noise_key = jax.random.fold_in(key, 12)
    drawn = jnp.clip(jax.random.normal(noise_key, (SLOTS, KVH * HD), jnp.float32), -4.0, 4.0)
    return drawn.astype(jnp.bfloat16)


def draw_values(key, part):
    noise_key = jax.random.fold_in(key, 13)
    scale_key = jax.random.fold_in(key, 31)
    head_ids = jnp.arange(KVH).astype(jnp.float32)
    ramp = 3.0 ** (head_ids / max(KVH - 1, 1))
    jitter = jnp.exp(jax.random.uniform(scale_key, (KVH,), jnp.float32, 0.0, jnp.log(2.0)))
    scales = ramp * jitter
    entries = jnp.clip(jax.random.normal(noise_key, (SLOTS, KVH * HD), jnp.float32), -4.0, 4.0)
    per_column = jnp.repeat(scales, HD)
    return (entries * per_column[None, :]).astype(jnp.bfloat16)


def draw_slot_pos(key, part):
    base_key = jax.random.fold_in(key, 14)
    shard_keys = jax.random.split(base_key, N_SEQ)

    def one_shard(shard_key):
        shuffled = jax.random.permutation(shard_key, TOK_DEV)
        return jnp.sort(shuffled[:CAP])
    return jax.vmap(one_shard)(shard_keys).reshape(SLOTS).astype(jnp.int32)


def block_scale(own_key, shape, shards, low, top_value):
    def one(dim, parts):
        draws = jax.random.uniform(jax.random.fold_in(jax.random.fold_in(own_key, 6), dim), (parts,), jnp.float32, low / len(shards), top_value / len(shards))
        return jnp.repeat(jnp.exp(draws), shape[dim] // parts).reshape((-1,) + (1,) * (len(shape) - dim - 1))

    factor_of = one(*shards[0])
    for cut in shards[1:]:
        factor_of = factor_of * one(*cut)
    return factor_of


def split_up(number_of, total, most, lean):
    loads = [(1 << 20) // math.isqrt(grade ** lean) + 1 for grade in range(2, number_of + 1)]
    surplus, given = total - most - (number_of - 1), [1] * (number_of - 1)
    while surplus > 0:
        movable = [i for i in range(number_of - 1) if given[i] < most]
        mass, remaining = sum([loads[i] for i in movable]), surplus
        for i in movable:
            addition = min(most - given[i], max(1, remaining * loads[i] // mass), surplus)
            given[i] = given[i] + addition
            surplus = surplus - addition
    return np.array([most] + given)


def uneven_parts(rng, count, total, bound, slope):
    if count == 2:
        one = jax.random.randint(rng, (), max(1, total - bound), min(bound, total - 1) + 1)
        return jnp.stack([one, total - one])
    tallies = jnp.asarray(split_up(count, total, bound, slope), jnp.int32)
    couples = (count - 1) // 2
    donor, taker = tallies[1:1 + 2 * couples:2], tallies[2:2 + 2 * couples:2]
    room = jnp.minimum(donor - 1, bound - taker)
    moved = jax.random.randint(jax.random.fold_in(rng, 1), (couples,), 0, 1 << 20) % (room + 1)
    tallies = tallies.at[1:1 + 2 * couples:2].set(donor - moved).at[2:2 + 2 * couples:2].set(taker + moved)
    return tallies[jax.random.permutation(jax.random.fold_in(rng, 2), count)]


def setup_inputs(seed: int = 0) -> dict:
    arg_keys = jax.random.split(jax.random.key(seed), 8)
    queries = draw_queries(jax.random.fold_in(arg_keys[7], 71), 0)
    keys = draw_keys(jax.random.fold_in(arg_keys[7], 71), 0)
    values = draw_values(jax.random.fold_in(arg_keys[7], 71), 0)
    router_prob = jnp.clip(0.2 + 0.8 * jax.random.uniform(arg_keys[3], (SLOTS,), jnp.float32) ** block_scale(arg_keys[3], (SLOTS,), ((0, 8),), -0.2, 0.2), 0.2, 1.0)
    norm_gain = jnp.clip(1.0 + 0.15 * jax.random.normal(arg_keys[4], (H * HD,), jnp.float32), 0.25, 1.75)
    slot_pos = draw_slot_pos(jax.random.fold_in(arg_keys[7], 71), 0)
    live_count = uneven_parts(arg_keys[6], N_SEQ, SELECTED, CAP, 2).astype(jnp.int32)
    return {"queries": queries, "keys": keys, "values": values, "router_prob": router_prob, "norm_gain": norm_gain, "slot_pos": slot_pos, "live_count": live_count}


def reference(queries, keys, values, router_prob, norm_gain, slot_pos, live_count):
    group_size = H // KVH
    limits = jnp.cumsum(live_count).astype(jnp.int32)
    starts = (limits - live_count).astype(jnp.int32)
    numbers = jnp.arange(SELECTED, dtype=jnp.int32)
    shard_of = lax.optimization_barrier(jnp.sum((limits[None, :] <= numbers[:, None]).astype(jnp.int32), axis=1)).astype(jnp.int32)
    slot_of = (numbers - starts[shard_of]).astype(jnp.int32)
    flat_index = (shard_of * CAP + slot_of).astype(jnp.int32)
    dense_queries = queries[flat_index].astype(jnp.float32)
    dense_keys = keys[flat_index].astype(jnp.float32)
    dense_values = values[flat_index]
    causal = numbers[:, None] >= numbers[None, :]
    score_scale = 1.0 / math.sqrt(HD)

    def one_head(head_number):
        kv_group = head_number // group_size
        query_head = lax.dynamic_slice_in_dim(dense_queries, head_number * HD, HD, 1)
        key_head = lax.dynamic_slice_in_dim(dense_keys, kv_group * HD, HD, 1)
        value_head = lax.dynamic_slice_in_dim(dense_values, kv_group * HD, HD, 1)
        scores = jnp.dot(query_head, key_head.T, precision=lax.Precision.HIGHEST) * score_scale
        scores = jnp.where(causal, scores, -jnp.inf)
        highest = lax.optimization_barrier(jnp.max(scores, axis=1, keepdims=True))
        weights = jnp.where(causal, jnp.exp(scores - highest), 0.0)
        totals = lax.optimization_barrier(jnp.sum(weights, axis=1, keepdims=True))
        summed = jnp.dot(weights.astype(jnp.bfloat16), value_head, preferred_element_type=jnp.float32)
        return (summed / totals).astype(jnp.bfloat16)
    heads = lax.map(one_head, jnp.arange(H, dtype=jnp.int32))
    attended = jnp.transpose(heads, (1, 0, 2)).reshape(SELECTED, H * HD)
    widened = attended.astype(jnp.float32)
    inverse = lax.rsqrt(lax.optimization_barrier(jnp.mean(widened * widened, axis=1)) + 1e-06)
    normed = router_prob[flat_index][:, None] * norm_gain[None, :] * widened * inverse[:, None]
    target_rows = (shard_of * TOK_DEV + slot_pos[flat_index]).astype(jnp.int32)
    routed = jnp.zeros((TOKENS, H * HD), jnp.bfloat16)
    return routed.at[target_rows].set(normed.astype(jnp.bfloat16))
```

```python
import functools
import math

import jax
import jax.numpy as jnp
from jax import lax
from jax.experimental import pallas as pl
from jax.experimental.pallas import tpu as pltpu
from jax.sharding import PartitionSpec as P

H = 32
HD = 128
TOK_DEV = 256


far_number = 1 << 30
epsilon = 1e-06
block_limit = 1024
lowest = -1e30


def attend_block(
    carried,
    current_key_block,
    value_block,
    key_numbers,
    head_grouped_rows,
    query_numbers,
    score_scale,
):
    highest, totals, running_output = carried
    scores = (
        jnp.einsum(
            "zpeo,jpo->pezj",
            head_grouped_rows,
            current_key_block,
            preferred_element_type=jnp.float32,
        )
        * score_scale
    )
    visible = key_numbers[None, None, None, :] <= query_numbers[None, None, :, None]
    masked = jnp.where(visible, scores, lowest)
    newest = jnp.maximum(highest, jnp.max(masked, axis=-1))
    weights = jnp.where(visible, jnp.exp(scores - newest[..., None]), 0.0)
    factor = jnp.exp(highest - newest)
    totals = totals * factor + jnp.sum(weights, axis=-1)
    update = jnp.einsum(
        "ycwh,hyu->ycwu",
        weights.astype(jnp.bfloat16),
        value_block,
        preferred_element_type=jnp.float32,
    )
    running_output = running_output * factor[..., None] + update
    return (newest, totals, running_output)


def fold_blocks(
    carried, key_all, value_all, head_grouped_rows, query_numbers, number_rule, score_scale
):
    length = key_all.shape[0]
    block_rows = min(length, block_limit)
    block_count = -(-length // block_rows)
    offsets = jnp.arange(block_count * block_rows, dtype=jnp.int32)
    numbers = jnp.where(offsets < length, number_rule(offsets), far_number)
    count_of_heads = key_all.shape[1] // HD
    key_blocks = key_all.reshape(block_count, block_rows, count_of_heads, HD)
    value_blocks = value_all.reshape(block_count, block_rows, count_of_heads, HD)
    total_block_count = numbers.reshape(block_count, block_rows)
    newest_query = jnp.max(query_numbers)

    def advance(running, blocks):
        current_key_block, value_block, key_numbers = blocks

        def unchanged(inside):
            return inside

        def updated(inside):
            return attend_block(
                inside,
                current_key_block,
                value_block,
                key_numbers,
                head_grouped_rows,
                query_numbers,
                score_scale,
            )

        running = lax.cond(jnp.min(key_numbers) > newest_query, unchanged, updated, running)
        return (running, None)

    carried, ignored = lax.scan(advance, carried, (key_blocks, value_blocks, total_block_count))
    return carried


def local(queries, keys, values, router_prob, norm_gain, slot_pos, live_count):
    device_mesh = lax.axis_size("seq")
    my_index = lax.axis_index("seq")
    capacity = queries.shape[0]
    local_heads = queries.shape[1] // HD
    local_groups = keys.shape[1] // HD
    group_size = local_heads // local_groups
    score_scale = 1.0 / math.sqrt(HD)
    counts = lax.all_gather(live_count, "seq", axis=0, tiled=True)
    limits = jnp.cumsum(counts)
    starts = limits - counts
    shard_range = jnp.arange(device_mesh, dtype=jnp.int32)
    self_hot = shard_range == my_index
    start_here = jnp.sum(jnp.where(self_hot, starts, 0))
    count_here = jnp.sum(jnp.where(self_hot, counts, 0))
    slot_index = jnp.arange(capacity, dtype=jnp.int32)

    def slot_numbers(positions):
        shard_id = positions // capacity
        within = positions % capacity
        one_hot = shard_id[:, None] == shard_range[None, :]
        begins = jnp.sum(jnp.where(one_hot, starts[None, :], 0), axis=1)
        surviving_token_count = jnp.sum(jnp.where(one_hot, counts[None, :], 0), axis=1)
        return jnp.where(within < surviving_token_count, begins + within, far_number)

    query_numbers = start_here + jnp.minimum(slot_index, count_here - 1)
    row_count = queries.shape[0]
    head_grouped_rows = queries.reshape(row_count, local_groups, group_size, HD)
    initial = (
        jnp.full((local_groups, group_size, row_count), lowest, jnp.float32),
        jnp.zeros((local_groups, group_size, row_count), jnp.float32),
        jnp.zeros((local_groups, group_size, row_count, HD), jnp.float32),
    )
    key_all, value_all = (
        lax.all_gather(keys, "seq", axis=0, tiled=True),
        lax.all_gather(values, "seq", axis=0, tiled=True),
    )
    highest, totals, running_output = fold_blocks(
        initial, key_all, value_all, head_grouped_rows, query_numbers, slot_numbers, score_scale
    )
    attended = (running_output / totals[..., None]).astype(jnp.bfloat16)
    attended = jnp.transpose(attended, (2, 0, 1, 3)).reshape(row_count, local_heads * HD)
    widened = attended.astype(jnp.float32)
    squares = jnp.sum(widened * widened, axis=1)
    total_squares = lax.psum(squares, "tp")
    inverse = lax.rsqrt(total_squares / (H * HD) + epsilon)
    normed = (router_prob[:, None] * norm_gain[None, :] * widened * inverse[:, None]).astype(
        jnp.bfloat16
    )
    alive = slot_index < count_here
    placer = (
        (jnp.arange(TOK_DEV, dtype=jnp.int32)[:, None] == slot_pos[None, :]) & alive[None, :]
    ).astype(jnp.bfloat16)
    return jnp.dot(placer, normed, preferred_element_type=jnp.float32).astype(jnp.bfloat16)


WIDTH = 2
KERNEL_SHARDS = 16
MESH = pl.DeviceIdType.MESH
FLAT = (((1,), (1,)), ((), ()))
TALL = (((0,), (0,)), ((), ()))


def kernel(
    shards,
    tp_size,
    q_hbm,
    k_hbm,
    v_hbm,
    prob_ref,
    gain_ref,
    pos_ref,
    count_ref,
    out_ref,
    q_buf,
    k_buf,
    v_buf,
    count_buf,
    high_ref,
    total_ref,
    acc_ref,
    att_ref,
    placed_ref,
    square_out,
    square_in,
    local_sem,
    send_sem,
    recv_sem,
    tp_send_sem,
    tp_recv_sem,
):
    me = lax.axis_index("seq")
    tp_me = lax.axis_index("tp")
    rows = shards // WIDTH
    row, column = me // WIDTH, lax.rem(me, WIDTH)
    beside = me + 1 - 2 * column
    groups, stacked, _ = q_buf.shape
    capacity = k_buf.shape[1]
    heads = stacked // capacity
    rate = math.log2(math.e) / math.sqrt(HD)

    local_copies = [
        pltpu.make_async_copy(k_hbm, k_buf.at[me], local_sem.at[0]),
        pltpu.make_async_copy(v_hbm, v_buf.at[me], local_sem.at[1]),
    ]
    for g in range(groups):
        for h in range(heads):
            local_copies.append(
                pltpu.make_async_copy(
                    q_hbm.at[:, pl.ds((g * heads + h) * HD, HD)],
                    q_buf.at[g, pl.ds(h * capacity, capacity), :],
                    local_sem.at[2 + g * heads + h],
                )
            )
    for copy in local_copies:
        copy.start()
    my_count = count_ref[0]
    count_buf[me] = jnp.full(count_buf.shape[1:], my_count, jnp.int32)
    square_out[...] = jnp.zeros_like(square_out)

    barrier = pltpu.get_barrier_semaphore()

    def greet(**where):
        pl.semaphore_signal(barrier, inc=1, device_id=where, device_id_type=MESH)

    greet(seq=beside)
    for step in range(1, tp_size):
        greet(tp=lax.rem(tp_me + step, tp_size))

    @pl.when(row > 0)
    def _():
        greet(seq=me - WIDTH)

    @pl.when(row < rows - 1)
    def _():
        greet(seq=me + WIDTH)

    pl.semaphore_wait(
        barrier,
        tp_size + jnp.where(row > 0, 1, 0) + jnp.where(row < rows - 1, 1, 0),
    )

    def piece_copy(kind, piece, way, back):
        buffer = (k_buf, v_buf, count_buf)[kind]
        source = buffer.at[piece]
        if back == 0 and kind < 2:
            source = (k_hbm, v_hbm)[kind]
        return pltpu.make_async_remote_copy(
            src_ref=source,
            dst_ref=buffer.at[piece],
            send_sem=send_sem.at[way, back, kind],
            recv_sem=recv_sem.at[piece, kind],
            device_id={"seq": (me + WIDTH, beside)[way]},
            device_id_type=MESH,
        )

    def send_piece(kinds, back, act):
        piece = me - WIDTH * back

        @pl.when(row < rows - 1)
        def _():
            for kind in kinds:
                act(piece_copy(kind, piece, 0, back))

        if back == 0:

            @pl.when(column == 0)
            def _():
                for kind in kinds:
                    act(piece_copy(kind, piece, 1, back))
        else:
            for kind in kinds:
                act(piece_copy(kind, piece, 1, back))

    def await_piece(piece, kinds):
        for kind in kinds:
            piece_copy(kind, piece, 0, 1).wait_recv()

    send_piece((2, 0, 1), 0, lambda copy: copy.start())

    def attend(keys, values, visible, first):
        for g in range(groups):
            lanes = slice(g * HD, (g + 1) * HD)
            scores = lax.dot_general(
                keys[:, lanes], q_buf[g], FLAT, preferred_element_type=jnp.float32
            )
            scores = jnp.where(visible, scores, lowest)
            newest = jnp.max(scores, axis=0, keepdims=True)
            if not first:
                highest = high_ref[g]
                newest = jnp.maximum(highest, newest)
            weights = jnp.exp2((scores - newest) * rate)
            total = jnp.sum(weights, axis=0, keepdims=True)
            update = lax.dot_general(
                values[:, lanes],
                weights.astype(jnp.bfloat16),
                TALL,
                preferred_element_type=jnp.float32,
            )
            if not first:
                factor = jnp.exp2((highest - newest) * rate)
                total = total + total_ref[g] * factor
                update = update + acc_ref[g] * factor
            high_ref[g] = newest
            total_ref[g] = total
            acc_ref[g] = update

    shape = (capacity, stacked)
    key_index = lax.broadcasted_iota(jnp.int32, shape, 0)
    query_index = lax.rem(lax.broadcasted_iota(jnp.int32, shape, 1), capacity)

    for copy in local_copies:
        copy.wait()
    attend(
        k_buf[me],
        v_buf[me],
        (key_index <= query_index) & (key_index < my_count),
        True,
    )

    def live(piece):
        limit = jnp.broadcast_to(count_buf[piece][:, :1], shape)
        return key_index < limit

    @pl.when(column == 1)
    def _():
        await_piece(me - 1, (2, 0, 1))
        attend(k_buf[me - 1], v_buf[me - 1], live(me - 1), False)

    token_shape = (out_ref.shape[0], capacity)
    chosen = (lax.broadcasted_iota(jnp.int32, token_shape, 0) == pos_ref[...]) & (
        lax.broadcasted_iota(jnp.int32, token_shape, 1) < my_count
    )

    def fold_row(back):
        low = WIDTH * (row - back)
        await_piece(beside - WIDTH * back, (2, 0, 1))
        attend(
            k_buf[pl.ds(low, WIDTH)].reshape(WIDTH * capacity, groups * HD),
            v_buf[pl.ds(low, WIDTH)].reshape(WIDTH * capacity, groups * HD),
            jnp.concatenate([live(low + i) for i in range(WIDTH)], axis=0),
            False,
        )

    for back in range(1, rows + 1):
        if back < rows:

            @pl.when(row >= back)
            def _(back=back):
                for kinds in ((2, 0), (1,)):
                    await_piece(me - WIDTH * back, kinds)
                    send_piece(kinds, back, lambda copy: copy.start())

        if back > 1:

            @pl.when(row >= back - 1)
            def _(back=back):
                fold_row(back - 1)

    squares = jnp.zeros((capacity, HD), jnp.float32)
    for g in range(groups):
        attended = (acc_ref[g] / total_ref[g]).T.astype(jnp.bfloat16)
        for h in range(heads):
            one = attended[h * capacity : (h + 1) * capacity]
            att_ref[:, (g * heads + h) * HD : (g * heads + h + 1) * HD] = one
            wide = one.astype(jnp.float32)
            squares = squares + wide * wide
    square_row = lax.dot_general(
        jnp.ones((8, HD), jnp.float32),
        squares,
        FLAT,
        precision=lax.Precision.HIGHEST,
        preferred_element_type=jnp.float32,
    )
    square_out[:, :capacity] = square_row
    tp_copies = []
    for step in range(1, tp_size):
        tp_copies.append(
            pltpu.make_async_remote_copy(
                src_ref=square_out,
                dst_ref=square_in.at[step - 1],
                send_sem=tp_send_sem.at[step - 1],
                recv_sem=tp_recv_sem.at[step - 1],
                device_id={"tp": lax.rem(tp_me + step, tp_size)},
                device_id_type=MESH,
            )
        )
    for copy in tp_copies:
        copy.start()

    placed_ref[...] = (
        jnp.dot(
            chosen.astype(jnp.float32).astype(jnp.bfloat16),
            att_ref[...],
            preferred_element_type=jnp.float32,
        )
        * gain_ref[...]
    )
    for copy in tp_copies:
        copy.wait()
    all_squares = square_row[:1]
    for step in range(1, tp_size):
        all_squares = all_squares + square_in[step - 1][:1, :capacity]
    inverse = lax.rsqrt(all_squares / (att_ref.shape[1] * tp_size) + epsilon)
    scale = jnp.sum(
        jnp.where(chosen, prob_ref[...] * inverse, 0.0), axis=1, keepdims=True
    )
    out_ref[...] = (placed_ref[...] * scale).astype(jnp.bfloat16)

    for back in range(rows):
        if back == 0:
            send_piece((2, 0, 1), 0, lambda copy: copy.wait_send())
        else:

            @pl.when(row >= back)
            def _(back=back):
                send_piece((2, 0, 1), back, lambda copy: copy.wait_send())


def local_kernel(queries, keys, values, router_prob, norm_gain, slot_pos, live_count):
    shards, tp_size = lax.axis_size("seq"), lax.axis_size("tp")
    capacity, width = queries.shape
    kv_width = keys.shape[1]
    groups = kv_width // HD
    stacked = width // kv_width * capacity
    rows = shards // WIDTH
    whole = pl.BlockSpec(memory_space=pltpu.VMEM)
    anywhere = pl.BlockSpec(memory_space=pl.ANY)
    return pl.pallas_call(
        functools.partial(kernel, shards, tp_size),
        out_shape=jax.ShapeDtypeStruct((TOK_DEV, width), jnp.bfloat16),
        in_specs=[
            anywhere,
            anywhere,
            anywhere,
            whole,
            whole,
            whole,
            pl.BlockSpec(memory_space=pltpu.SMEM),
        ],
        out_specs=whole,
        scratch_shapes=[
            pltpu.VMEM((groups, stacked, HD), jnp.bfloat16),
            pltpu.VMEM((shards, capacity, kv_width), jnp.bfloat16),
            pltpu.VMEM((shards, capacity, kv_width), jnp.bfloat16),
            pltpu.VMEM((shards, 1, HD), jnp.int32),
            pltpu.VMEM((groups, 1, stacked), jnp.float32),
            pltpu.VMEM((groups, 1, stacked), jnp.float32),
            pltpu.VMEM((groups, HD, stacked), jnp.float32),
            pltpu.VMEM((capacity, width), jnp.bfloat16),
            pltpu.VMEM((TOK_DEV, width), jnp.float32),
            pltpu.VMEM((8, 128), jnp.float32),
            pltpu.VMEM((tp_size, 8, 128), jnp.float32),
            pltpu.SemaphoreType.DMA((2 + width // HD,)),
            pltpu.SemaphoreType.DMA((2, rows, 3)),
            pltpu.SemaphoreType.DMA((shards, 3)),
            pltpu.SemaphoreType.DMA((tp_size,)),
            pltpu.SemaphoreType.DMA((tp_size,)),
        ],
        compiler_params=pltpu.CompilerParams(collective_id=0, has_side_effects=True),
    )(
        queries,
        keys,
        values,
        router_prob.reshape(1, -1),
        norm_gain.reshape(1, -1),
        slot_pos.reshape(1, -1),
        live_count,
    )


def solution(mesh):
    in_specs = (
        P("seq", "tp"),
        P("seq", "tp"),
        P("seq", "tp"),
        P("seq"),
        P("tp"),
        P("seq"),
        P("seq"),
    )
    out_specs = P("seq", "tp")
    shards = mesh.shape["seq"]
    one_kernel = shards % WIDTH == 0 and shards <= KERNEL_SHARDS
    body = local_kernel if one_kernel else local
    return jax.shard_map(body, mesh=mesh, in_specs=in_specs, out_specs=out_specs, check_vma=False)
```

```python
import functools
import math

import jax
import jax.numpy as jnp
from jax import lax
from jax.experimental import pallas as pl
from jax.experimental.pallas import tpu as pltpu
from jax.sharding import PartitionSpec as P

H = 32
HD = 128
TOK_DEV = 256


far_number = 1 << 30
epsilon = 1e-06
block_limit = 1024
lowest = -1e30


def attend_block(
    carried,
    current_key_block,
    value_block,
    key_numbers,
    head_grouped_rows,
    query_numbers,
    score_scale,
):
    highest, totals, running_output = carried
    scores = (
        jnp.einsum(
            "zpeo,jpo->pezj",
            head_grouped_rows,
            current_key_block,
            preferred_element_type=jnp.float32,
        )
        * score_scale
    )
    visible = key_numbers[None, None, None, :] <= query_numbers[None, None, :, None]
    masked = jnp.where(visible, scores, lowest)
    newest = jnp.maximum(highest, jnp.max(masked, axis=-1))
    weights = jnp.where(visible, jnp.exp(scores - newest[..., None]), 0.0)
    factor = jnp.exp(highest - newest)
    totals = totals * factor + jnp.sum(weights, axis=-1)
    update = jnp.einsum(
        "ycwh,hyu->ycwu",
        weights.astype(jnp.bfloat16),
        value_block,
        preferred_element_type=jnp.float32,
    )
    running_output = running_output * factor[..., None] + update
    return (newest, totals, running_output)


def fold_blocks(
    carried, key_all, value_all, head_grouped_rows, query_numbers, number_rule, score_scale
):
    length = key_all.shape[0]
    block_rows = min(length, block_limit)
    block_count = -(-length // block_rows)
    offsets = jnp.arange(block_count * block_rows, dtype=jnp.int32)
    numbers = jnp.where(offsets < length, number_rule(offsets), far_number)
    count_of_heads = key_all.shape[1] // HD
    key_blocks = key_all.reshape(block_count, block_rows, count_of_heads, HD)
    value_blocks = value_all.reshape(block_count, block_rows, count_of_heads, HD)
    total_block_count = numbers.reshape(block_count, block_rows)
    newest_query = jnp.max(query_numbers)

    def advance(running, blocks):
        current_key_block, value_block, key_numbers = blocks

        def unchanged(inside):
            return inside

        def updated(inside):
            return attend_block(
                inside,
                current_key_block,
                value_block,
                key_numbers,
                head_grouped_rows,
                query_numbers,
                score_scale,
            )

        running = lax.cond(jnp.min(key_numbers) > newest_query, unchanged, updated, running)
        return (running, None)

    carried, ignored = lax.scan(advance, carried, (key_blocks, value_blocks, total_block_count))
    return carried


def local(queries, keys, values, router_prob, norm_gain, slot_pos, live_count):
    device_mesh = lax.axis_size("seq")
    my_index = lax.axis_index("seq")
    capacity = queries.shape[0]
    local_heads = queries.shape[1] // HD
    local_groups = keys.shape[1] // HD
    group_size = local_heads // local_groups
    score_scale = 1.0 / math.sqrt(HD)
    counts = lax.all_gather(live_count, "seq", axis=0, tiled=True)
    limits = jnp.cumsum(counts)
    starts = limits - counts
    shard_range = jnp.arange(device_mesh, dtype=jnp.int32)
    self_hot = shard_range == my_index
    start_here = jnp.sum(jnp.where(self_hot, starts, 0))
    count_here = jnp.sum(jnp.where(self_hot, counts, 0))
    slot_index = jnp.arange(capacity, dtype=jnp.int32)

    def slot_numbers(positions):
        shard_id = positions // capacity
        within = positions % capacity
        one_hot = shard_id[:, None] == shard_range[None, :]
        begins = jnp.sum(jnp.where(one_hot, starts[None, :], 0), axis=1)
        surviving_token_count = jnp.sum(jnp.where(one_hot, counts[None, :], 0), axis=1)
        return jnp.where(within < surviving_token_count, begins + within, far_number)

    query_numbers = start_here + jnp.minimum(slot_index, count_here - 1)
    row_count = queries.shape[0]
    head_grouped_rows = queries.reshape(row_count, local_groups, group_size, HD)
    initial = (
        jnp.full((local_groups, group_size, row_count), lowest, jnp.float32),
        jnp.zeros((local_groups, group_size, row_count), jnp.float32),
        jnp.zeros((local_groups, group_size, row_count, HD), jnp.float32),
    )
    key_all, value_all = (
        lax.all_gather(keys, "seq", axis=0, tiled=True),
        lax.all_gather(values, "seq", axis=0, tiled=True),
    )
    highest, totals, running_output = fold_blocks(
        initial, key_all, value_all, head_grouped_rows, query_numbers, slot_numbers, score_scale
    )
    attended = (running_output / totals[..., None]).astype(jnp.bfloat16)
    attended = jnp.transpose(attended, (2, 0, 1, 3)).reshape(row_count, local_heads * HD)
    widened = attended.astype(jnp.float32)
    squares = jnp.sum(widened * widened, axis=1)
    total_squares = lax.psum(squares, "tp")
    inverse = lax.rsqrt(total_squares / (H * HD) + epsilon)
    normed = (router_prob[:, None] * norm_gain[None, :] * widened * inverse[:, None]).astype(
        jnp.bfloat16
    )
    alive = slot_index < count_here
    placer = (
        (jnp.arange(TOK_DEV, dtype=jnp.int32)[:, None] == slot_pos[None, :]) & alive[None, :]
    ).astype(jnp.bfloat16)
    return jnp.dot(placer, normed, preferred_element_type=jnp.float32).astype(jnp.bfloat16)


WIDTH = 2
CHUNKS = 1
VMEM_BYTES = 16 << 20
ROW_BLOCKS = 1
KERNEL_SHARDS = 16
MESH = pl.DeviceIdType.MESH
FLAT = (((1,), (1,)), ((), ()))
TALL = (((0,), (0,)), ((), ()))


def kernel(
    shards,
    tp_size,
    q_hbm,
    k_hbm,
    v_hbm,
    prob_hbm,
    count_hbm,
    att_ref,
    scale_ref,
    q_buf,
    k_buf,
    v_buf,
    count_buf,
    high_ref,
    total_ref,
    acc_ref,
    square_out,
    square_in,
    prob_ref,
    count_ref,
    local_sem,
    send_sem,
    recv_sem,
    tp_send_sem,
    tp_recv_sem,
):
    me = lax.axis_index("seq")
    tp_me = lax.axis_index("tp")
    rows = shards // WIDTH
    row, column = me // WIDTH, lax.rem(me, WIDTH)
    beside = me + 1 - 2 * column
    groups, stacked, _ = q_buf.shape
    capacity = k_buf.shape[1]
    heads = stacked // capacity
    rate = math.log2(math.e) / math.sqrt(HD)

    count_copy = pltpu.make_async_copy(count_hbm, count_ref, local_sem.at[0])
    count_copy.start()
    small_copies = [
        pltpu.make_async_copy(prob_hbm, prob_ref, local_sem.at[1]),
    ]
    local_copies = [
        pltpu.make_async_copy(k_hbm, k_buf.at[me], local_sem.at[4]),
        pltpu.make_async_copy(v_hbm, v_buf.at[me], local_sem.at[5]),
    ]
    for g in range(groups):
        for h in range(heads):
            local_copies.append(
                pltpu.make_async_copy(
                    q_hbm.at[:, pl.ds((g * heads + h) * HD, HD)],
                    q_buf.at[g, pl.ds(h * capacity, capacity), :],
                    local_sem.at[6 + g * heads + h],
                )
            )

    barrier = pltpu.get_barrier_semaphore()

    def greet(**where):
        pl.semaphore_signal(barrier, inc=1, device_id=where, device_id_type=MESH)

    greet(seq=beside)
    for step in range(1, tp_size):
        greet(tp=lax.rem(tp_me + step, tp_size))

    met = tp_size
    for hop in range(1, rows, 2):

        @pl.when(row >= hop)
        def _(hop=hop):
            greet(seq=me - WIDTH * hop)

        @pl.when(row < rows - hop)
        def _(hop=hop):
            greet(seq=me + WIDTH * hop)

        met = met + jnp.where(row >= hop, 1, 0) + jnp.where(row < rows - hop, 1, 0)

    for copy in local_copies + small_copies:
        copy.start()
    count_copy.wait()
    my_count = count_ref[0]
    count_buf[me] = jnp.full(count_buf.shape[1:], my_count, jnp.int32)
    square_out[...] = jnp.zeros_like(square_out)
    pl.semaphore_wait(barrier, met)

    length = capacity // CHUNKS
    parts = [(count_buf, None, slice(0, 1))]
    for buffer, own in ((k_buf, k_hbm), (v_buf, v_hbm)):
        for chunk in range(CHUNKS):
            parts.append((buffer, own, pl.ds(chunk * length, length)))

    def part_copy(part, piece, hop, back):
        buffer, own, span = parts[part]
        target = buffer.at[piece, span]
        source = target
        return pltpu.make_async_remote_copy(
            src_ref=source,
            dst_ref=target,
            send_sem=send_sem.at[hop, back, part],
            recv_sem=recv_sem.at[piece, part],
            device_id={"seq": me + WIDTH * hop if hop else beside},
            device_id_type=MESH,
        )

    def each_target(back, act):
        hops = range(1, rows, 2) if back == 0 else (1,) if back % 2 else ()
        for hop in hops:

            @pl.when(row < rows - hop)
            def _(hop=hop):
                act(hop)

            if hop == 1:
                each_beside(back, act)
        if not hops:
            each_beside(back, act)

    def each_beside(back, act):
        if back == 0:

            @pl.when(column == 0)
            def _():
                act(0)
        else:
            act(0)

    def await_piece(piece):
        for part in range(len(parts)):
            part_copy(part, piece, 0, 1).wait_recv()

    def send_own(hop):
        for part in range(len(parts)):
            part_copy(part, me, hop, 0).start()

    for copy in local_copies[:2]:
        copy.wait()
    each_target(0, send_own)

    def relay(back):
        piece = me - WIDTH * back
        for part in range(len(parts)):
            part_copy(part, piece, 0, 1).wait_recv()
            each_target(back, lambda hop: part_copy(part, piece, hop, back).start())

    def attend(keys, values, visible, first):
        for g in range(groups):
            lanes = slice(g * HD, (g + 1) * HD)
            scores = lax.dot_general(
                keys[:, lanes], q_buf[g], FLAT, preferred_element_type=jnp.float32
            )
            scores = jnp.where(visible, scores, lowest)
            newest = jnp.max(scores, axis=0, keepdims=True)
            if not first:
                highest = high_ref[g]
                newest = jnp.maximum(highest, newest)
            weights = jnp.exp2((scores - newest) * rate)
            total = jnp.sum(weights, axis=0, keepdims=True)
            update = lax.dot_general(
                values[:, lanes],
                weights.astype(jnp.bfloat16),
                TALL,
                preferred_element_type=jnp.float32,
            )
            if not first:
                factor = jnp.exp2((highest - newest) * rate)
                total = total + total_ref[g] * factor
                update = update + acc_ref[g] * factor
            high_ref[g] = newest
            total_ref[g] = total
            acc_ref[g] = update

    shape = (capacity, stacked)
    key_index = lax.broadcasted_iota(jnp.int32, shape, 0)
    query_index = lax.rem(lax.broadcasted_iota(jnp.int32, shape, 1), capacity)

    for copy in local_copies[2:]:
        copy.wait()
    attend(
        k_buf[me],
        v_buf[me],
        (key_index <= query_index) & (key_index < my_count),
        True,
    )

    def live(piece):
        limit = jnp.broadcast_to(count_buf[piece][:, :1], shape)
        return key_index < limit

    def fold_beside():
        @pl.when(column == 1)
        def _():
            await_piece(me - 1)
            attend(k_buf[me - 1], v_buf[me - 1], live(me - 1), False)

    for copy in small_copies:
        copy.wait()

    def fold_row(back):
        low = WIDTH * (row - back)
        await_piece(beside - WIDTH * back)
        attend(
            k_buf[pl.ds(low, WIDTH)].reshape(WIDTH * capacity, groups * HD),
            v_buf[pl.ds(low, WIDTH)].reshape(WIDTH * capacity, groups * HD),
            jnp.concatenate([live(low + i) for i in range(WIDTH)], axis=0),
            False,
        )

    for back in range(1, rows + 1):
        if back < rows:

            @pl.when(row >= back)
            def _(back=back):
                relay(back)

        if back == 1:
            fold_beside()
        else:

            @pl.when(row >= back - 1)
            def _(back=back):
                fold_row(back - 1)

    squares = jnp.zeros((capacity, HD), jnp.float32)
    for g in range(groups):
        attended = (acc_ref[g] / total_ref[g]).T.astype(jnp.bfloat16)
        for h in range(heads):
            one = attended[h * capacity : (h + 1) * capacity]
            att_ref[:, (g * heads + h) * HD : (g * heads + h + 1) * HD] = one
            wide = one.astype(jnp.float32)
            squares = squares + wide * wide
    square_row = lax.dot_general(
        jnp.ones((8, HD), jnp.float32),
        squares,
        FLAT,
        precision=lax.Precision.HIGHEST,
        preferred_element_type=jnp.float32,
    )
    square_out[:, :capacity] = square_row
    tp_copies = []
    for step in range(1, tp_size):
        tp_copies.append(
            pltpu.make_async_remote_copy(
                src_ref=square_out,
                dst_ref=square_in.at[step - 1],
                send_sem=tp_send_sem.at[step - 1],
                recv_sem=tp_recv_sem.at[step - 1],
                device_id={"tp": lax.rem(tp_me + step, tp_size)},
                device_id_type=MESH,
            )
        )
    for copy in tp_copies:
        copy.start()

    for copy in tp_copies:
        copy.wait()
    all_squares = square_row[:1]
    for step in range(1, tp_size):
        all_squares = all_squares + square_in[step - 1][:1, :capacity]
    inverse = lax.rsqrt(all_squares / (att_ref.shape[1] * tp_size) + epsilon)
    scale_ref[:, :capacity] = jnp.broadcast_to(
        prob_ref[...] * inverse, (scale_ref.shape[0], capacity)
    )

    def settle(back):
        def wait(hop):
            for part in range(len(parts)):
                part_copy(part, me - WIDTH * back, hop, back).wait_send()

        each_target(back, wait)

    settle(0)
    for back in range(1, rows):

        @pl.when(row >= back)
        def _(back=back):
            settle(back)


def place_kernel(att_ref, scale_ref, gain_ref, pos_ref, count_ref, out_ref):
    shape = (out_ref.shape[0], att_ref.shape[0])
    first = pl.program_id(0) * shape[0]
    chosen = (lax.broadcasted_iota(jnp.int32, shape, 0) + first == pos_ref[...]) & (
        lax.broadcasted_iota(jnp.int32, shape, 1) < count_ref[0]
    )
    placed = jnp.dot(
        chosen.astype(jnp.float32).astype(jnp.bfloat16),
        att_ref[...],
        preferred_element_type=jnp.float32,
    )
    scale = jnp.sum(
        jnp.where(chosen, scale_ref[:1, : shape[1]], 0.0), axis=1, keepdims=True
    )
    out_ref[...] = (placed * gain_ref[...] * scale).astype(jnp.bfloat16)


def local_kernel(queries, keys, values, router_prob, norm_gain, slot_pos, live_count):
    shards, tp_size = lax.axis_size("seq"), lax.axis_size("tp")
    capacity, width = queries.shape
    kv_width = keys.shape[1]
    groups = kv_width // HD
    stacked = width // kv_width * capacity
    rows = shards // WIDTH
    whole = pl.BlockSpec(memory_space=pltpu.VMEM)
    anywhere = pl.BlockSpec(memory_space=pltpu.HBM)
    attended, scale = pl.pallas_call(
        functools.partial(kernel, shards, tp_size),
        out_shape=(
            pltpu.VMEM((capacity, width), jnp.bfloat16),
            pltpu.VMEM((8, 128), jnp.float32),
        ),
        in_specs=[
            anywhere,
            anywhere,
            anywhere,
            anywhere,
            anywhere,
        ],
        out_specs=(whole, whole),
        scratch_shapes=[
            pltpu.VMEM((groups, stacked, HD), jnp.bfloat16),
            pltpu.VMEM((shards, capacity, kv_width), jnp.bfloat16),
            pltpu.VMEM((shards, capacity, kv_width), jnp.bfloat16),
            pltpu.VMEM((shards, 1, HD), jnp.int32),
            pltpu.VMEM((groups, 1, stacked), jnp.float32),
            pltpu.VMEM((groups, 1, stacked), jnp.float32),
            pltpu.VMEM((groups, HD, stacked), jnp.float32),
            pltpu.VMEM((8, 128), jnp.float32),
            pltpu.VMEM((tp_size, 8, 128), jnp.float32),
            pltpu.VMEM((1, capacity), jnp.float32),
            pltpu.SMEM((1,), jnp.int32),
            pltpu.SemaphoreType.DMA((6 + width // HD,)),
            pltpu.SemaphoreType.DMA((rows, rows, 1 + 2 * CHUNKS)),
            pltpu.SemaphoreType.DMA((shards, 1 + 2 * CHUNKS)),
            pltpu.SemaphoreType.DMA((tp_size,)),
            pltpu.SemaphoreType.DMA((tp_size,)),
        ],
        compiler_params=pltpu.CompilerParams(
            collective_id=0, has_side_effects=True
        ),
    )(
        queries,
        keys,
        values,
        router_prob.reshape(1, -1),
        live_count,
    )
    block = TOK_DEV // ROW_BLOCKS
    return pl.pallas_call(
        place_kernel,
        grid=(ROW_BLOCKS,),
        out_shape=jax.ShapeDtypeStruct((TOK_DEV, width), jnp.bfloat16),
        in_specs=[
            whole,
            whole,
            whole,
            whole,
            pl.BlockSpec(memory_space=pltpu.SMEM),
        ],
        out_specs=pl.BlockSpec((block, width), lambda i: (i, 0)),
        compiler_params=pltpu.CompilerParams(vmem_limit_bytes=VMEM_BYTES),
        name="place",
    )(attended, scale, norm_gain.reshape(1, -1), slot_pos.reshape(1, -1), live_count)


def solution(mesh):
    in_specs = (
        P("seq", "tp"),
        P("seq", "tp"),
        P("seq", "tp"),
        P("seq"),
        P("tp"),
        P("seq"),
        P("seq"),
    )
    out_specs = P("seq", "tp")
    shards = mesh.shape["seq"]
    one_kernel = shards % WIDTH == 0 and shards <= KERNEL_SHARDS
    body = local_kernel if one_kernel else local
    return jax.shard_map(body, mesh=mesh, in_specs=in_specs, out_specs=out_specs, check_vma=False)
```

```python
import functools
import math

import jax
import jax.numpy as jnp
from jax import lax
from jax.experimental import pallas as pl
from jax.experimental.pallas import tpu as pltpu
from jax.sharding import PartitionSpec as P

H = 32
HD = 128
TOK_DEV = 256


far_number = 1 << 30
epsilon = 1e-06
block_limit = 1024
lowest = -1e30


def attend_block(
    carried,
    current_key_block,
    value_block,
    key_numbers,
    head_grouped_rows,
    query_numbers,
    score_scale,
):
    highest, totals, running_output = carried
    scores = (
        jnp.einsum(
            "zpeo,jpo->pezj",
            head_grouped_rows,
            current_key_block,
            preferred_element_type=jnp.float32,
        )
        * score_scale
    )
    visible = key_numbers[None, None, None, :] <= query_numbers[None, None, :, None]
    masked = jnp.where(visible, scores, lowest)
    newest = jnp.maximum(highest, jnp.max(masked, axis=-1))
    weights = jnp.where(visible, jnp.exp(scores - newest[..., None]), 0.0)
    factor = jnp.exp(highest - newest)
    totals = totals * factor + jnp.sum(weights, axis=-1)
    update = jnp.einsum(
        "ycwh,hyu->ycwu",
        weights.astype(jnp.bfloat16),
        value_block,
        preferred_element_type=jnp.float32,
    )
    running_output = running_output * factor[..., None] + update
    return (newest, totals, running_output)


def fold_blocks(
    carried, key_all, value_all, head_grouped_rows, query_numbers, number_rule, score_scale
):
    length = key_all.shape[0]
    block_rows = min(length, block_limit)
    block_count = -(-length // block_rows)
    offsets = jnp.arange(block_count * block_rows, dtype=jnp.int32)
    numbers = jnp.where(offsets < length, number_rule(offsets), far_number)
    count_of_heads = key_all.shape[1] // HD
    key_blocks = key_all.reshape(block_count, block_rows, count_of_heads, HD)
    value_blocks = value_all.reshape(block_count, block_rows, count_of_heads, HD)
    total_block_count = numbers.reshape(block_count, block_rows)
    newest_query = jnp.max(query_numbers)

    def advance(running, blocks):
        current_key_block, value_block, key_numbers = blocks

        def unchanged(inside):
            return inside

        def updated(inside):
            return attend_block(
                inside,
                current_key_block,
                value_block,
                key_numbers,
                head_grouped_rows,
                query_numbers,
                score_scale,
            )

        running = lax.cond(jnp.min(key_numbers) > newest_query, unchanged, updated, running)
        return (running, None)

    carried, ignored = lax.scan(advance, carried, (key_blocks, value_blocks, total_block_count))
    return carried


def local(queries, keys, values, router_prob, norm_gain, slot_pos, live_count):
    device_mesh = lax.axis_size("seq")
    my_index = lax.axis_index("seq")
    capacity = queries.shape[0]
    local_heads = queries.shape[1] // HD
    local_groups = keys.shape[1] // HD
    group_size = local_heads // local_groups
    score_scale = 1.0 / math.sqrt(HD)
    counts = lax.all_gather(live_count, "seq", axis=0, tiled=True)
    limits = jnp.cumsum(counts)
    starts = limits - counts
    shard_range = jnp.arange(device_mesh, dtype=jnp.int32)
    self_hot = shard_range == my_index
    start_here = jnp.sum(jnp.where(self_hot, starts, 0))
    count_here = jnp.sum(jnp.where(self_hot, counts, 0))
    slot_index = jnp.arange(capacity, dtype=jnp.int32)

    def slot_numbers(positions):
        shard_id = positions // capacity
        within = positions % capacity
        one_hot = shard_id[:, None] == shard_range[None, :]
        begins = jnp.sum(jnp.where(one_hot, starts[None, :], 0), axis=1)
        surviving_token_count = jnp.sum(jnp.where(one_hot, counts[None, :], 0), axis=1)
        return jnp.where(within < surviving_token_count, begins + within, far_number)

    query_numbers = start_here + jnp.minimum(slot_index, count_here - 1)
    row_count = queries.shape[0]
    head_grouped_rows = queries.reshape(row_count, local_groups, group_size, HD)
    initial = (
        jnp.full((local_groups, group_size, row_count), lowest, jnp.float32),
        jnp.zeros((local_groups, group_size, row_count), jnp.float32),
        jnp.zeros((local_groups, group_size, row_count, HD), jnp.float32),
    )
    key_all, value_all = (
        lax.all_gather(keys, "seq", axis=0, tiled=True),
        lax.all_gather(values, "seq", axis=0, tiled=True),
    )
    highest, totals, running_output = fold_blocks(
        initial, key_all, value_all, head_grouped_rows, query_numbers, slot_numbers, score_scale
    )
    attended = (running_output / totals[..., None]).astype(jnp.bfloat16)
    attended = jnp.transpose(attended, (2, 0, 1, 3)).reshape(row_count, local_heads * HD)
    widened = attended.astype(jnp.float32)
    squares = jnp.sum(widened * widened, axis=1)
    total_squares = lax.psum(squares, "tp")
    inverse = lax.rsqrt(total_squares / (H * HD) + epsilon)
    normed = (router_prob[:, None] * norm_gain[None, :] * widened * inverse[:, None]).astype(
        jnp.bfloat16
    )
    alive = slot_index < count_here
    placer = (
        (jnp.arange(TOK_DEV, dtype=jnp.int32)[:, None] == slot_pos[None, :]) & alive[None, :]
    ).astype(jnp.bfloat16)
    return jnp.dot(placer, normed, preferred_element_type=jnp.float32).astype(jnp.bfloat16)


WIDTH = 2
CHUNKS = 1
VMEM_BYTES = 16 << 20
ROW_BLOCKS = 1
KERNEL_SHARDS = 16
MESH = pl.DeviceIdType.MESH
FLAT = (((1,), (1,)), ((), ()))
TALL = (((0,), (0,)), ((), ()))


def kernel(
    shards,
    tp_size,
    q_hbm,
    k_hbm,
    v_hbm,
    prob_hbm,
    count_hbm,
    att_ref,
    scale_ref,
    q_buf,
    k_buf,
    v_buf,
    count_buf,
    high_ref,
    total_ref,
    acc_ref,
    square_out,
    square_in,
    prob_ref,
    count_ref,
    local_sem,
    send_sem,
    recv_sem,
    tp_send_sem,
    tp_recv_sem,
):
    me = lax.axis_index("seq")
    tp_me = lax.axis_index("tp")
    rows = shards // WIDTH
    row, column = me // WIDTH, lax.rem(me, WIDTH)
    beside = me + 1 - 2 * column
    groups, stacked, _ = q_buf.shape
    capacity = k_buf.shape[1]
    heads = stacked // capacity
    rate = math.log2(math.e) / math.sqrt(HD)

    count_copy = pltpu.make_async_copy(count_hbm, count_ref, local_sem.at[0])
    count_copy.start()
    small_copies = [
        pltpu.make_async_copy(prob_hbm, prob_ref, local_sem.at[1]),
    ]
    local_copies = [
        pltpu.make_async_copy(k_hbm, k_buf.at[me], local_sem.at[4]),
        pltpu.make_async_copy(v_hbm, v_buf.at[me], local_sem.at[5]),
    ]
    for g in range(groups):
        for h in range(heads):
            local_copies.append(
                pltpu.make_async_copy(
                    q_hbm.at[:, pl.ds((g * heads + h) * HD, HD)],
                    q_buf.at[g, pl.ds(h * capacity, capacity), :],
                    local_sem.at[6 + g * heads + h],
                )
            )

    barrier = pltpu.get_barrier_semaphore()

    def greet(**where):
        pl.semaphore_signal(barrier, inc=1, device_id=where, device_id_type=MESH)

    greet(seq=beside)
    for step in range(1, tp_size):
        greet(tp=lax.rem(tp_me + step, tp_size))

    met = tp_size
    for hop in (1,):

        @pl.when(row >= hop)
        def _(hop=hop):
            greet(seq=me - WIDTH * hop)

        @pl.when(row < rows - hop)
        def _(hop=hop):
            greet(seq=me + WIDTH * hop)

        met = met + jnp.where(row >= hop, 1, 0) + jnp.where(row < rows - hop, 1, 0)

    for copy in local_copies + small_copies:
        copy.start()
    count_copy.wait()
    my_count = count_ref[0]
    count_buf[me] = jnp.full(count_buf.shape[1:], my_count, jnp.int32)
    square_out[...] = jnp.zeros_like(square_out)
    pl.semaphore_wait(barrier, met)

    length = capacity // CHUNKS
    parts = [(count_buf, None, slice(0, 1))]
    for buffer, own in ((k_buf, k_hbm), (v_buf, v_hbm)):
        for chunk in range(CHUNKS):
            parts.append((buffer, own, pl.ds(chunk * length, length)))

    def part_copy(part, piece, hop, back):
        buffer, own, span = parts[part]
        target = buffer.at[piece, span]
        source = target
        return pltpu.make_async_remote_copy(
            src_ref=source,
            dst_ref=target,
            send_sem=send_sem.at[hop, back, part],
            recv_sem=recv_sem.at[piece, part],
            device_id={"seq": me + WIDTH * hop if hop else beside},
            device_id_type=MESH,
        )

    def each_target(back, act):
        hops = (1,) if back == 0 else (1,)
        for hop in hops:

            @pl.when(row < rows - hop)
            def _(hop=hop):
                act(hop)

            if hop == 1:
                each_beside(back, act)
        if not hops:
            each_beside(back, act)

    def each_beside(back, act):
        if back == 0:

            @pl.when(column == 0)
            def _():
                act(0)
        else:
            act(0)

    def await_piece(piece):
        for part in range(len(parts)):
            part_copy(part, piece, 0, 1).wait_recv()

    def send_own(hop):
        for part in range(len(parts)):
            part_copy(part, me, hop, 0).start()

    for copy in local_copies[:2]:
        copy.wait()
    each_target(0, send_own)

    def relay(back):
        piece = me - WIDTH * back
        for part in range(len(parts)):
            part_copy(part, piece, 0, 1).wait_recv()
            each_target(back, lambda hop: part_copy(part, piece, hop, back).start())

    def attend(keys, values, visible, first):
        for g in range(groups):
            lanes = slice(g * HD, (g + 1) * HD)
            scores = lax.dot_general(
                keys[:, lanes], q_buf[g], FLAT, preferred_element_type=jnp.float32
            )
            scores = jnp.where(visible, scores, lowest)
            newest = jnp.max(scores, axis=0, keepdims=True)
            if not first:
                highest = high_ref[g]
                newest = jnp.maximum(highest, newest)
            weights = jnp.exp2((scores - newest) * rate)
            total = jnp.sum(weights, axis=0, keepdims=True)
            update = lax.dot_general(
                values[:, lanes],
                weights.astype(jnp.bfloat16),
                TALL,
                preferred_element_type=jnp.float32,
            )
            if not first:
                factor = jnp.exp2((highest - newest) * rate)
                total = total + total_ref[g] * factor
                update = update + acc_ref[g] * factor
            high_ref[g] = newest
            total_ref[g] = total
            acc_ref[g] = update

    shape = (capacity, stacked)
    key_index = lax.broadcasted_iota(jnp.int32, shape, 0)
    query_index = lax.rem(lax.broadcasted_iota(jnp.int32, shape, 1), capacity)

    for copy in local_copies[2:]:
        copy.wait()
    attend(
        k_buf[me],
        v_buf[me],
        (key_index <= query_index) & (key_index < my_count),
        True,
    )

    def live(piece):
        limit = jnp.broadcast_to(count_buf[piece][:, :1], shape)
        return key_index < limit

    def fold_beside():
        @pl.when(column == 1)
        def _():
            await_piece(me - 1)
            attend(k_buf[me - 1], v_buf[me - 1], live(me - 1), False)

    for copy in small_copies:
        copy.wait()

    def fold_row(back):
        low = WIDTH * (row - back)
        await_piece(beside - WIDTH * back)
        attend(
            k_buf[pl.ds(low, WIDTH)].reshape(WIDTH * capacity, groups * HD),
            v_buf[pl.ds(low, WIDTH)].reshape(WIDTH * capacity, groups * HD),
            jnp.concatenate([live(low + i) for i in range(WIDTH)], axis=0),
            False,
        )

    for back in range(1, rows + 1):
        if back < rows:

            @pl.when(row >= back)
            def _(back=back):
                relay(back)

        if back == 1:
            fold_beside()
        else:

            @pl.when(row >= back - 1)
            def _(back=back):
                fold_row(back - 1)

    squares = jnp.zeros((capacity, HD), jnp.float32)
    for g in range(groups):
        attended = (acc_ref[g] / total_ref[g]).T.astype(jnp.bfloat16)
        for h in range(heads):
            one = attended[h * capacity : (h + 1) * capacity]
            att_ref[:, (g * heads + h) * HD : (g * heads + h + 1) * HD] = one
            wide = one.astype(jnp.float32)
            squares = squares + wide * wide
    square_row = lax.dot_general(
        jnp.ones((8, HD), jnp.float32),
        squares,
        FLAT,
        precision=lax.Precision.HIGHEST,
        preferred_element_type=jnp.float32,
    )
    square_out[:, :capacity] = square_row
    tp_copies = []
    for step in range(1, tp_size):
        tp_copies.append(
            pltpu.make_async_remote_copy(
                src_ref=square_out,
                dst_ref=square_in.at[step - 1],
                send_sem=tp_send_sem.at[step - 1],
                recv_sem=tp_recv_sem.at[step - 1],
                device_id={"tp": lax.rem(tp_me + step, tp_size)},
                device_id_type=MESH,
            )
        )
    for copy in tp_copies:
        copy.start()

    for copy in tp_copies:
        copy.wait()
    all_squares = square_row[:1]
    for step in range(1, tp_size):
        all_squares = all_squares + square_in[step - 1][:1, :capacity]
    inverse = lax.rsqrt(all_squares / (att_ref.shape[1] * tp_size) + epsilon)
    scale_ref[:, :capacity] = jnp.broadcast_to(
        prob_ref[...] * inverse, (scale_ref.shape[0], capacity)
    )

    def settle(back):
        def wait(hop):
            for part in range(len(parts)):
                part_copy(part, me - WIDTH * back, hop, back).wait_send()

        each_target(back, wait)

    settle(0)
    for back in range(1, rows):

        @pl.when(row >= back)
        def _(back=back):
            settle(back)


def place_kernel(att_ref, scale_ref, gain_ref, pos_ref, count_ref, out_ref):
    shape = (out_ref.shape[0], att_ref.shape[0])
    first = pl.program_id(0) * shape[0]
    chosen = (lax.broadcasted_iota(jnp.int32, shape, 0) + first == pos_ref[...]) & (
        lax.broadcasted_iota(jnp.int32, shape, 1) < count_ref[0]
    )
    placed = jnp.dot(
        chosen.astype(jnp.float32).astype(jnp.bfloat16),
        att_ref[...],
        preferred_element_type=jnp.float32,
    )
    scale = jnp.sum(
        jnp.where(chosen, scale_ref[:1, : shape[1]], 0.0), axis=1, keepdims=True
    )
    out_ref[...] = (placed * gain_ref[...] * scale).astype(jnp.bfloat16)


def local_kernel(queries, keys, values, router_prob, norm_gain, slot_pos, live_count):
    shards, tp_size = lax.axis_size("seq"), lax.axis_size("tp")
    capacity, width = queries.shape
    kv_width = keys.shape[1]
    groups = kv_width // HD
    stacked = width // kv_width * capacity
    rows = shards // WIDTH
    whole = pl.BlockSpec(memory_space=pltpu.VMEM)
    anywhere = pl.BlockSpec(memory_space=pltpu.HBM)
    attended, scale = pl.pallas_call(
        functools.partial(kernel, shards, tp_size),
        out_shape=(
            pltpu.VMEM((capacity, width), jnp.bfloat16),
            pltpu.VMEM((8, 128), jnp.float32),
        ),
        in_specs=[
            anywhere,
            anywhere,
            anywhere,
            anywhere,
            anywhere,
        ],
        out_specs=(whole, whole),
        scratch_shapes=[
            pltpu.VMEM((groups, stacked, HD), jnp.bfloat16),
            pltpu.VMEM((shards, capacity, kv_width), jnp.bfloat16),
            pltpu.VMEM((shards, capacity, kv_width), jnp.bfloat16),
            pltpu.VMEM((shards, 1, HD), jnp.int32),
            pltpu.VMEM((groups, 1, stacked), jnp.float32),
            pltpu.VMEM((groups, 1, stacked), jnp.float32),
            pltpu.VMEM((groups, HD, stacked), jnp.float32),
            pltpu.VMEM((8, 128), jnp.float32),
            pltpu.VMEM((tp_size, 8, 128), jnp.float32),
            pltpu.VMEM((1, capacity), jnp.float32),
            pltpu.SMEM((1,), jnp.int32),
            pltpu.SemaphoreType.DMA((6 + width // HD,)),
            pltpu.SemaphoreType.DMA((rows, rows, 1 + 2 * CHUNKS)),
            pltpu.SemaphoreType.DMA((shards, 1 + 2 * CHUNKS)),
            pltpu.SemaphoreType.DMA((tp_size,)),
            pltpu.SemaphoreType.DMA((tp_size,)),
        ],
        compiler_params=pltpu.CompilerParams(
            collective_id=0, has_side_effects=True
        ),
    )(
        queries,
        keys,
        values,
        router_prob.reshape(1, -1),
        live_count,
    )
    block = TOK_DEV // ROW_BLOCKS
    return pl.pallas_call(
        place_kernel,
        grid=(ROW_BLOCKS,),
        out_shape=jax.ShapeDtypeStruct((TOK_DEV, width), jnp.bfloat16),
        in_specs=[
            whole,
            whole,
            whole,
            whole,
            pl.BlockSpec(memory_space=pltpu.SMEM),
        ],
        out_specs=pl.BlockSpec((block, width), lambda i: (i, 0)),
        compiler_params=pltpu.CompilerParams(vmem_limit_bytes=VMEM_BYTES),
        name="place",
    )(attended, scale, norm_gain.reshape(1, -1), slot_pos.reshape(1, -1), live_count)


def solution(mesh):
    in_specs = (
        P("seq", "tp"),
        P("seq", "tp"),
        P("seq", "tp"),
        P("seq"),
        P("tp"),
        P("seq"),
        P("seq"),
    )
    out_specs = P("seq", "tp")
    shards = mesh.shape["seq"]
    one_kernel = shards % WIDTH == 0 and shards <= KERNEL_SHARDS
    body = local_kernel if one_kernel else local
    return jax.shard_map(body, mesh=mesh, in_specs=in_specs, out_specs=out_specs, check_vma=False)
```

```python
import functools
import math

import jax
import jax.numpy as jnp
from jax import lax
from jax.experimental import pallas as pl
from jax.experimental.pallas import tpu as pltpu
from jax.sharding import PartitionSpec as P

H = 32
HD = 128
TOK_DEV = 256


far_number = 1 << 30
epsilon = 1e-06
block_limit = 1024
lowest = -1e30


def attend_block(
    carried,
    current_key_block,
    value_block,
    key_numbers,
    head_grouped_rows,
    query_numbers,
    score_scale,
):
    highest, totals, running_output = carried
    scores = (
        jnp.einsum(
            "zpeo,jpo->pezj",
            head_grouped_rows,
            current_key_block,
            preferred_element_type=jnp.float32,
        )
        * score_scale
    )
    visible = key_numbers[None, None, None, :] <= query_numbers[None, None, :, None]
    masked = jnp.where(visible, scores, lowest)
    newest = jnp.maximum(highest, jnp.max(masked, axis=-1))
    weights = jnp.where(visible, jnp.exp(scores - newest[..., None]), 0.0)
    factor = jnp.exp(highest - newest)
    totals = totals * factor + jnp.sum(weights, axis=-1)
    update = jnp.einsum(
        "ycwh,hyu->ycwu",
        weights.astype(jnp.bfloat16),
        value_block,
        preferred_element_type=jnp.float32,
    )
    running_output = running_output * factor[..., None] + update
    return (newest, totals, running_output)


def fold_blocks(
    carried, key_all, value_all, head_grouped_rows, query_numbers, number_rule, score_scale
):
    length = key_all.shape[0]
    block_rows = min(length, block_limit)
    block_count = -(-length // block_rows)
    offsets = jnp.arange(block_count * block_rows, dtype=jnp.int32)
    numbers = jnp.where(offsets < length, number_rule(offsets), far_number)
    count_of_heads = key_all.shape[1] // HD
    key_blocks = key_all.reshape(block_count, block_rows, count_of_heads, HD)
    value_blocks = value_all.reshape(block_count, block_rows, count_of_heads, HD)
    total_block_count = numbers.reshape(block_count, block_rows)
    newest_query = jnp.max(query_numbers)

    def advance(running, blocks):
        current_key_block, value_block, key_numbers = blocks

        def unchanged(inside):
            return inside

        def updated(inside):
            return attend_block(
                inside,
                current_key_block,
                value_block,
                key_numbers,
                head_grouped_rows,
                query_numbers,
                score_scale,
            )

        running = lax.cond(jnp.min(key_numbers) > newest_query, unchanged, updated, running)
        return (running, None)

    carried, ignored = lax.scan(advance, carried, (key_blocks, value_blocks, total_block_count))
    return carried


def local(queries, keys, values, router_prob, norm_gain, slot_pos, live_count):
    device_mesh = lax.axis_size("seq")
    my_index = lax.axis_index("seq")
    capacity = queries.shape[0]
    local_heads = queries.shape[1] // HD
    local_groups = keys.shape[1] // HD
    group_size = local_heads // local_groups
    score_scale = 1.0 / math.sqrt(HD)
    counts = lax.all_gather(live_count, "seq", axis=0, tiled=True)
    limits = jnp.cumsum(counts)
    starts = limits - counts
    shard_range = jnp.arange(device_mesh, dtype=jnp.int32)
    self_hot = shard_range == my_index
    start_here = jnp.sum(jnp.where(self_hot, starts, 0))
    count_here = jnp.sum(jnp.where(self_hot, counts, 0))
    slot_index = jnp.arange(capacity, dtype=jnp.int32)

    def slot_numbers(positions):
        shard_id = positions // capacity
        within = positions % capacity
        one_hot = shard_id[:, None] == shard_range[None, :]
        begins = jnp.sum(jnp.where(one_hot, starts[None, :], 0), axis=1)
        surviving_token_count = jnp.sum(jnp.where(one_hot, counts[None, :], 0), axis=1)
        return jnp.where(within < surviving_token_count, begins + within, far_number)

    query_numbers = start_here + jnp.minimum(slot_index, count_here - 1)
    row_count = queries.shape[0]
    head_grouped_rows = queries.reshape(row_count, local_groups, group_size, HD)
    initial = (
        jnp.full((local_groups, group_size, row_count), lowest, jnp.float32),
        jnp.zeros((local_groups, group_size, row_count), jnp.float32),
        jnp.zeros((local_groups, group_size, row_count, HD), jnp.float32),
    )
    key_all, value_all = (
        lax.all_gather(keys, "seq", axis=0, tiled=True),
        lax.all_gather(values, "seq", axis=0, tiled=True),
    )
    highest, totals, running_output = fold_blocks(
        initial, key_all, value_all, head_grouped_rows, query_numbers, slot_numbers, score_scale
    )
    attended = (running_output / totals[..., None]).astype(jnp.bfloat16)
    attended = jnp.transpose(attended, (2, 0, 1, 3)).reshape(row_count, local_heads * HD)
    widened = attended.astype(jnp.float32)
    squares = jnp.sum(widened * widened, axis=1)
    total_squares = lax.psum(squares, "tp")
    inverse = lax.rsqrt(total_squares / (H * HD) + epsilon)
    normed = (router_prob[:, None] * norm_gain[None, :] * widened * inverse[:, None]).astype(
        jnp.bfloat16
    )
    alive = slot_index < count_here
    placer = (
        (jnp.arange(TOK_DEV, dtype=jnp.int32)[:, None] == slot_pos[None, :]) & alive[None, :]
    ).astype(jnp.bfloat16)
    return jnp.dot(placer, normed, preferred_element_type=jnp.float32).astype(jnp.bfloat16)


WIDTH = 2
CHUNKS = 1
VMEM_BYTES = 16 << 20
ROW_BLOCKS = 1
KERNEL_SHARDS = 16
MESH = pl.DeviceIdType.MESH
FLAT = (((1,), (1,)), ((), ()))
TALL = (((0,), (0,)), ((), ()))


def kernel(
    shards,
    tp_size,
    q_hbm,
    k_hbm,
    v_hbm,
    prob_hbm,
    count_hbm,
    att_ref,
    scale_ref,
    q_buf,
    k_buf,
    v_buf,
    count_buf,
    high_ref,
    total_ref,
    acc_ref,
    square_out,
    square_in,
    prob_ref,
    count_ref,
    local_sem,
    send_sem,
    recv_sem,
    tp_send_sem,
    tp_recv_sem,
):
    me = lax.axis_index("seq")
    tp_me = lax.axis_index("tp")
    rows = shards // WIDTH
    row, column = me // WIDTH, lax.rem(me, WIDTH)
    beside = me + 1 - 2 * column
    groups, stacked, _ = q_buf.shape
    capacity = k_buf.shape[1]
    heads = stacked // capacity
    rate = math.log2(math.e) / math.sqrt(HD)

    count_copy = pltpu.make_async_copy(count_hbm, count_ref, local_sem.at[0])
    count_copy.start()
    small_copies = [
        pltpu.make_async_copy(prob_hbm, prob_ref, local_sem.at[1]),
    ]
    local_copies = [
        pltpu.make_async_copy(k_hbm, k_buf.at[me], local_sem.at[4]),
        pltpu.make_async_copy(v_hbm, v_buf.at[me], local_sem.at[5]),
    ]
    for g in range(groups):
        for h in range(heads):
            local_copies.append(
                pltpu.make_async_copy(
                    q_hbm.at[:, pl.ds((g * heads + h) * HD, HD)],
                    q_buf.at[g, pl.ds(h * capacity, capacity), :],
                    local_sem.at[6 + g * heads + h],
                )
            )

    for copy in local_copies + small_copies:
        copy.start()

    barrier = pltpu.get_barrier_semaphore()

    def greet(**where):
        pl.semaphore_signal(barrier, inc=1, device_id=where, device_id_type=MESH)

    greet(seq=beside)
    for step in range(1, tp_size):
        greet(tp=lax.rem(tp_me + step, tp_size))

    met = tp_size
    @pl.when(row > 0)
    def _():
        greet(seq=me - WIDTH)
        greet(seq=beside - WIDTH)

    @pl.when(row < rows - 1)
    def _():
        greet(seq=me + WIDTH)
        greet(seq=beside + WIDTH)

    met = met + jnp.where(row > 0, 2, 0) + jnp.where(row < rows - 1, 2, 0)

    count_copy.wait()
    my_count = count_ref[0]
    count_buf[me] = jnp.full(count_buf.shape[1:], my_count, jnp.int32)
    square_out[...] = jnp.zeros_like(square_out)
    pl.semaphore_wait(barrier, met)

    length = capacity // CHUNKS
    parts = [(count_buf, None, slice(0, 1))]
    for buffer, own in ((k_buf, k_hbm), (v_buf, v_hbm)):
        for chunk in range(CHUNKS):
            parts.append((buffer, own, pl.ds(chunk * length, length)))

    def part_copy(part, piece, hop, back):
        buffer, own, span = parts[part]
        target = buffer.at[piece, span]
        source = target
        return pltpu.make_async_remote_copy(
            src_ref=source,
            dst_ref=target,
            send_sem=send_sem.at[hop, back, part],
            recv_sem=recv_sem.at[piece, part],
            device_id={"seq": (beside, me + WIDTH, beside + WIDTH)[hop]},
            device_id_type=MESH,
        )

    def each_target(back, act):
        @pl.when(row < rows - 1)
        def _():
            act(1)

        @pl.when((row < rows - 1) & (row == back))
        def _():
            act(2)

        if back == 0:

            @pl.when(column == 0)
            def _():
                act(0)
        else:

            @pl.when(row != back)
            def _():
                act(0)

    def await_piece(piece):
        for part in range(len(parts)):
            part_copy(part, piece, 0, 1).wait_recv()

    def send_own(hop):
        for part in range(len(parts)):
            part_copy(part, me, hop, 0).start()

    for copy in local_copies[:2]:
        copy.wait()
    each_target(0, send_own)

    def relay(back):
        piece = me - WIDTH * back
        for part in range(len(parts)):
            part_copy(part, piece, 0, 1).wait_recv()
            each_target(back, lambda hop: part_copy(part, piece, hop, back).start())

    def attend(keys, values, visible, first):
        for g in range(groups):
            lanes = slice(g * HD, (g + 1) * HD)
            scores = lax.dot_general(
                keys[:, lanes], q_buf[g], FLAT, preferred_element_type=jnp.float32
            )
            scores = jnp.where(visible, scores, lowest)
            newest = jnp.max(scores, axis=0, keepdims=True)
            if not first:
                highest = high_ref[g]
                newest = jnp.maximum(highest, newest)
            weights = jnp.exp2((scores - newest) * rate)
            total = jnp.sum(weights, axis=0, keepdims=True)
            update = lax.dot_general(
                values[:, lanes],
                weights.astype(jnp.bfloat16),
                TALL,
                preferred_element_type=jnp.float32,
            )
            if not first:
                factor = jnp.exp2((highest - newest) * rate)
                total = total + total_ref[g] * factor
                update = update + acc_ref[g] * factor
            high_ref[g] = newest
            total_ref[g] = total
            acc_ref[g] = update

    shape = (capacity, stacked)
    key_index = lax.broadcasted_iota(jnp.int32, shape, 0)
    query_index = lax.rem(lax.broadcasted_iota(jnp.int32, shape, 1), capacity)

    for copy in local_copies[2:]:
        copy.wait()
    attend(
        k_buf[me],
        v_buf[me],
        (key_index <= query_index) & (key_index < my_count),
        True,
    )

    def live(piece):
        limit = jnp.broadcast_to(count_buf[piece][:, :1], shape)
        return key_index < limit

    def fold_beside():
        @pl.when(column == 1)
        def _():
            await_piece(me - 1)
            attend(k_buf[me - 1], v_buf[me - 1], live(me - 1), False)

    for copy in small_copies:
        copy.wait()

    def fold_row(back):
        low = WIDTH * (row - back)
        await_piece(beside - WIDTH * back)
        attend(
            k_buf[pl.ds(low, WIDTH)].reshape(WIDTH * capacity, groups * HD),
            v_buf[pl.ds(low, WIDTH)].reshape(WIDTH * capacity, groups * HD),
            jnp.concatenate([live(low + i) for i in range(WIDTH)], axis=0),
            False,
        )

    for back in range(1, rows + 1):
        if back < rows:

            @pl.when(row >= back)
            def _(back=back):
                relay(back)

        if back == 1:
            fold_beside()
        else:

            @pl.when(row >= back - 1)
            def _(back=back):
                fold_row(back - 1)

    squares = jnp.zeros((capacity, HD), jnp.float32)
    for g in range(groups):
        attended = (acc_ref[g] / total_ref[g]).T.astype(jnp.bfloat16)
        for h in range(heads):
            one = attended[h * capacity : (h + 1) * capacity]
            att_ref[:, (g * heads + h) * HD : (g * heads + h + 1) * HD] = one
            wide = one.astype(jnp.float32)
            squares = squares + wide * wide
    square_row = lax.dot_general(
        jnp.ones((8, HD), jnp.float32),
        squares,
        FLAT,
        precision=lax.Precision.HIGHEST,
        preferred_element_type=jnp.float32,
    )
    square_out[:, :capacity] = square_row
    tp_copies = []
    for step in range(1, tp_size):
        tp_copies.append(
            pltpu.make_async_remote_copy(
                src_ref=square_out,
                dst_ref=square_in.at[step - 1],
                send_sem=tp_send_sem.at[step - 1],
                recv_sem=tp_recv_sem.at[step - 1],
                device_id={"tp": lax.rem(tp_me + step, tp_size)},
                device_id_type=MESH,
            )
        )
    for copy in tp_copies:
        copy.start()

    for copy in tp_copies:
        copy.wait()
    all_squares = square_row[:1]
    for step in range(1, tp_size):
        all_squares = all_squares + square_in[step - 1][:1, :capacity]
    inverse = lax.rsqrt(all_squares / (att_ref.shape[1] * tp_size) + epsilon)
    scale_ref[:, :capacity] = jnp.broadcast_to(
        prob_ref[...] * inverse, (scale_ref.shape[0], capacity)
    )

    def settle(back):
        def wait(hop):
            for part in range(len(parts)):
                part_copy(part, me - WIDTH * back, hop, back).wait_send()

        each_target(back, wait)

    settle(0)
    for back in range(1, rows):

        @pl.when(row >= back)
        def _(back=back):
            settle(back)


def place_kernel(att_ref, scale_ref, gain_ref, pos_ref, count_ref, out_ref):
    shape = (out_ref.shape[0], att_ref.shape[0])
    first = pl.program_id(0) * shape[0]
    chosen = (lax.broadcasted_iota(jnp.int32, shape, 0) + first == pos_ref[...]) & (
        lax.broadcasted_iota(jnp.int32, shape, 1) < count_ref[0]
    )
    placed = jnp.dot(
        chosen.astype(jnp.float32).astype(jnp.bfloat16),
        att_ref[...],
        preferred_element_type=jnp.float32,
    )
    scale = jnp.sum(
        jnp.where(chosen, scale_ref[:1, : shape[1]], 0.0), axis=1, keepdims=True
    )
    out_ref[...] = (placed * gain_ref[...] * scale).astype(jnp.bfloat16)


def local_kernel(queries, keys, values, router_prob, norm_gain, slot_pos, live_count):
    shards, tp_size = lax.axis_size("seq"), lax.axis_size("tp")
    capacity, width = queries.shape
    kv_width = keys.shape[1]
    groups = kv_width // HD
    stacked = width // kv_width * capacity
    rows = shards // WIDTH
    whole = pl.BlockSpec(memory_space=pltpu.VMEM)
    anywhere = pl.BlockSpec(memory_space=pltpu.HBM)
    attended, scale = pl.pallas_call(
        functools.partial(kernel, shards, tp_size),
        out_shape=(
            pltpu.VMEM((capacity, width), jnp.bfloat16),
            pltpu.VMEM((8, 128), jnp.float32),
        ),
        in_specs=[
            anywhere,
            anywhere,
            anywhere,
            anywhere,
            anywhere,
        ],
        out_specs=(whole, whole),
        scratch_shapes=[
            pltpu.VMEM((groups, stacked, HD), jnp.bfloat16),
            pltpu.VMEM((shards, capacity, kv_width), jnp.bfloat16),
            pltpu.VMEM((shards, capacity, kv_width), jnp.bfloat16),
            pltpu.VMEM((shards, 1, HD), jnp.int32),
            pltpu.VMEM((groups, 1, stacked), jnp.float32),
            pltpu.VMEM((groups, 1, stacked), jnp.float32),
            pltpu.VMEM((groups, HD, stacked), jnp.float32),
            pltpu.VMEM((8, 128), jnp.float32),
            pltpu.VMEM((tp_size, 8, 128), jnp.float32),
            pltpu.VMEM((1, capacity), jnp.float32),
            pltpu.SMEM((1,), jnp.int32),
            pltpu.SemaphoreType.DMA((6 + width // HD,)),
            pltpu.SemaphoreType.DMA((3, rows, 1 + 2 * CHUNKS)),
            pltpu.SemaphoreType.DMA((shards, 1 + 2 * CHUNKS)),
            pltpu.SemaphoreType.DMA((tp_size,)),
            pltpu.SemaphoreType.DMA((tp_size,)),
        ],
        compiler_params=pltpu.CompilerParams(
            collective_id=0, has_side_effects=True
        ),
    )(
        queries,
        keys,
        values,
        router_prob.reshape(1, -1),
        live_count,
    )
    block = TOK_DEV // ROW_BLOCKS
    return pl.pallas_call(
        place_kernel,
        grid=(ROW_BLOCKS,),
        out_shape=jax.ShapeDtypeStruct((TOK_DEV, width), jnp.bfloat16),
        in_specs=[
            whole,
            whole,
            whole,
            whole,
            pl.BlockSpec(memory_space=pltpu.SMEM),
        ],
        out_specs=pl.BlockSpec((block, width), lambda i: (i, 0)),
        compiler_params=pltpu.CompilerParams(vmem_limit_bytes=VMEM_BYTES),
        name="place",
    )(attended, scale, norm_gain.reshape(1, -1), slot_pos.reshape(1, -1), live_count)


def solution(mesh):
    in_specs = (
        P("seq", "tp"),
        P("seq", "tp"),
        P("seq", "tp"),
        P("seq"),
        P("tp"),
        P("seq"),
        P("seq"),
    )
    out_specs = P("seq", "tp")
    shards = mesh.shape["seq"]
    one_kernel = shards % WIDTH == 0 and shards <= KERNEL_SHARDS
    body = local_kernel if one_kernel else local
    return jax.shard_map(body, mesh=mesh, in_specs=in_specs, out_specs=out_specs, check_vma=False)
```
